32 devices in a mesh: gx: 4 (over x, core), gy: 2 (over y), gz: 4 (over z).
Axes of the slice: x: 2, y: 2, z: 4, core: 2. Of those that a mesh axis runs over, the one named last changes fastest.
Arguments:
- hidden_rows: bfloat16 [4096, 5120], P(('gx', 'gy', 'gz')), may hold values from -12 to 12
- query_grad: bfloat16 [4096, 5120], P(('gx', 'gy', 'gz')), may hold values from -384 to 384
- value_grad: bfloat16 [4096, 5120], P(('gx', 'gy', 'gz')), may hold values from -384 to 384
- query_down: bfloat16 [16, 5120], replicated, may hold values from -0.078125 to 0.078125
- query_up: bfloat16 [16, 5120], replicated, may hold values from -0.078125 to 0.078125
- value_down: bfloat16 [16, 5120], replicated, may hold values from -0.078125 to 0.078125
- value_up: bfloat16 [16, 5120], replicated, may hold values from -0.078125 to 0.078125
- lengths: int32 [64], P(('gx', 'gy', 'gz')), may hold values from 8 to 64, as said below
Outputs:
- grad_query_down: float32 [16, 5120], replicated
- grad_query_up: float32 [16, 5120], replicated
- grad_value_down: float32 [16, 5120], replicated
- grad_value_up: float32 [16, 5120], replicated
The draws below stay inside these ranges and needn't reach their ends.
Inputs may be any that keep to these rules, and one draw needn't show every extreme that they name: `lengths`: the last sequence has 64 valid tokens and the first one 64 // 8.
All inputs are finite; a program needn't handle non-finite values.
Results may differ from the reference program's by a relative error of at most 0.0031.
Values sent between devices are 32-bit elements; how exact they have to be, the bound alone decides.
No kernel may reach another device: no remote copies, remote signals or barrier semaphores. Data moves between devices by JAX's collectives and lax.ppermute only.
A program may use at most 64 MiB of HBM per device.

```python
import jax
import jax.numpy as jnp
from jax import lax

D = 5120
RANK = 16
SEQ = 64
SEQS_DEV = 2
NSEQ = 64
TOKENS = 4096


def draw_lengths(key, part):
    owner = jnp.arange(NSEQ, dtype=jnp.int32) // SEQS_DEV
    span = max(NSEQ // SEQS_DEV - 1, 1)
    lowest = SEQ // 4
    base = lowest + owner * (SEQ - lowest) // span
    jitter = jax.random.randint(key, (NSEQ,), -(SEQ // 8), SEQ // 8 + 1, dtype=jnp.int32)
    values = jnp.clip(base + jitter, SEQ // 8, SEQ)
    values = values.at[NSEQ - 1].set(SEQ)
    values = values.at[0].set(SEQ // 8)
    return values.astype(jnp.int32)


def with_spikes(result, own_key, source, target, parts, factor):
    def block_of(dim):
        return (jnp.arange(result.shape[dim]) // (result.shape[dim] // parts)).reshape((-1,) + (1,) * (result.ndim - 1 - dim))

    one_side = jax.random.permutation(own_key, parts)[block_of(target)]
    far = (block_of(target) + parts // 2) % parts
    return jnp.where((block_of(source) == one_side) | (block_of(source) == far), factor * result, result)


def block_levels(rng, extent, pieces, least, high):
    def one(position, blocks):
        steps = jax.random.uniform(jax.random.fold_in(jax.random.fold_in(rng, 6), position), (blocks,), jnp.float32, least / len(pieces), high / len(pieces))
        return jnp.repeat(jnp.exp(steps), extent[position] // blocks).reshape((-1,) + (1,) * (len(extent) - position - 1))

    level = one(*pieces[0])
    for cut in pieces[1:]:
        level = level * one(*cut)
    return level


def gaussian(stream_key, extent, spread, limit, pieces=(), held_as=jnp.bfloat16):
    factor_of = block_levels(stream_key, extent, pieces, -0.22, 0.18) if pieces else 1.0
    drawn = jax.random.normal(stream_key, extent, jnp.float32) * spread * factor_of
    return jnp.minimum(jnp.maximum(drawn, -limit), limit).astype(held_as)


def gaussian_with(key, dims, spread, reach, split, heavy, kind=jnp.bfloat16):
    array = spread * jax.random.normal(key, dims, jnp.float32)
    if split:
        array = array * block_levels(key, dims, split, -0.22, 0.18)
    return jnp.clip(with_spikes(array, jax.random.fold_in(key, 3), *heavy), -reach, reach).astype(kind)


def setup_inputs(seed: int = 0) -> dict:
    keys = jax.random.split(jax.random.key(seed), 9)
    hidden_rows = gaussian_with(keys[0], (TOKENS, D), 1.0, 12.0, ((0, 32),), (0, 1, 32, 2.75))
    query_grad = gaussian_with(keys[1], (TOKENS, D), (0.5 * TOKENS ** 0.5), 384.0, ((0, 32),), (0, 1, 32, 2.75))
    value_grad = gaussian_with(keys[2], (TOKENS, D), (0.5 * TOKENS ** 0.5), 384.0, ((0, 32),), (0, 1, 32, 2.75))
    query_down = gaussian(keys[3], (RANK, D), D ** -0.5, 0.078125)
    query_up = gaussian(keys[4], (RANK, D), D ** -0.5, 0.078125)
    value_down = gaussian(keys[5], (RANK, D), D ** -0.5, 0.078125)
    value_up = gaussian(keys[6], (RANK, D), D ** -0.5, 0.078125)
    lengths = draw_lengths(jax.random.fold_in(keys[8], 71), 0)
    return {"hidden_rows": hidden_rows, "query_grad": query_grad, "value_grad": value_grad, "query_down": query_down, "query_up": query_up, "value_down": value_down, "value_up": value_up, "lengths": lengths}


def adapter_sums(rows, grad_out, down, up, valid):
    inner = lax.dot_general(rows, down, (((1,), (1,)), ((), ())), preferred_element_type=jnp.float32)
    inner = jnp.where(valid[:, None], inner, 0.0).astype(jnp.bfloat16)
    back = lax.dot_general(grad_out, up, (((1,), (1,)), ((), ())), preferred_element_type=jnp.float32)
    back = jnp.where(valid[:, None], back, 0.0).astype(jnp.bfloat16)
    up_sum = lax.dot_general(inner, grad_out, (((0,), (0,)), ((), ())), preferred_element_type=jnp.float32)
    down_sum = lax.dot_general(back, rows, (((0,), (0,)), ((), ())), preferred_element_type=jnp.float32)
    return down_sum, up_sum


def reference(hidden_rows, query_grad, value_grad, query_down, query_up, value_down, value_up, lengths):
    slots = jnp.arange(SEQ, dtype=jnp.int32)
    valid = (slots[None, :] < lengths[:, None]).reshape(-1)
    total = jnp.sum(lengths.astype(jnp.float32))
    q_down, q_up = adapter_sums(hidden_rows, query_grad, query_down, query_up, valid)
    v_down, v_up = adapter_sums(hidden_rows, value_grad, value_down, value_up, valid)
    return q_down / total, q_up / total, v_down / total, v_up / total
```

```python
import jax
import jax.numpy as jnp
from jax import lax
from jax.sharding import PartitionSpec as P

AXES = ("gx", "gy", "gz")
LANES = 128
SUBLANES = 8


def adapter_sums(rows, grad_out, down, up, valid):
    inner = lax.dot_general(
        rows, down, (((1,), (1,)), ((), ())), preferred_element_type=jnp.float32
    )
    inner = jnp.where(valid[:, None], inner, 0.0).astype(jnp.bfloat16)
    back = lax.dot_general(
        grad_out, up, (((1,), (1,)), ((), ())), preferred_element_type=jnp.float32
    )
    back = jnp.where(valid[:, None], back, 0.0).astype(jnp.bfloat16)
    up_sum = lax.dot_general(
        inner, grad_out, (((0,), (0,)), ((), ())), preferred_element_type=jnp.float32
    )
    down_sum = lax.dot_general(
        back, rows, (((0,), (0,)), ((), ())), preferred_element_type=jnp.float32
    )
    return down_sum, up_sum


def axis_bits(axis, size, first=0):
    bits = size.bit_length() - 1
    assert size == 1 << bits
    return [(axis, 1 << k) for k in range(first, bits)]


class Swaps:
    def __init__(self, sizes):
        self.sizes = sizes
        near = axis_bits("gx", sizes["gx"], 1) + axis_bits("gy", sizes["gy"])
        far = axis_bits("gz", sizes["gz"])
        self.orders = (near + far, self.paired(near) + self.paired(far))
        self.at = {axis: lax.axis_index(axis) for axis in AXES}
        self.core = self.at["gx"] & 1

    @staticmethod
    def paired(bits):
        order = list(bits)
        for k in range(0, len(order) - 1, 2):
            order[k], order[k + 1] = order[k + 1], order[k]
        return order

    def count(self):
        return len(self.orders[0])

    def high(self, stage):
        flags = [(self.at[axis] & bit) != 0 for axis, bit in (order[stage] for order in self.orders)]
        return jnp.where(self.core == 0, flags[0], flags[1])

    def swap(self, stage, array):
        gx, gy, gz = (self.sizes[axis] for axis in AXES)
        pairs = []
        for i in range(gx):
            for j in range(gy):
                for k in range(gz):
                    place = {"gx": i, "gy": j, "gz": k}
                    axis, bit = self.orders[i & 1][stage]
                    place[axis] ^= bit
                    there = (place["gx"] * gy + place["gy"]) * gz + place["gz"]
                    pairs.append(((i * gy + j) * gz + k, there))
        return lax.ppermute(array, AXES, pairs)

    def swap_cores(self, array):
        return lax.ppermute(array, "gx", [(i, i ^ 1) for i in range(self.sizes["gx"])])


def body(sizes, hidden_rows, query_grad, value_grad, query_down, query_up, value_down, value_up, lengths):
    seq_len = hidden_rows.shape[0] // lengths.shape[0]
    slots = jnp.arange(seq_len, dtype=jnp.int32)
    valid = (slots[None, :] < lengths[:, None]).reshape(-1)
    local_count = jnp.sum(lengths.astype(jnp.float32))
    rank_dim, width = query_down.shape
    swaps = Swaps(sizes)
    tail = jnp.full((2 * rank_dim, LANES), local_count, jnp.float32)

    def sums(grad_out, down, up):
        pair = jnp.concatenate(adapter_sums(hidden_rows, grad_out, down, up, valid), axis=0)
        return jnp.concatenate([pair, tail], axis=1)

    query = sums(query_grad, query_down, query_up)
    value = sums(value_grad, value_down, value_up)
    core = swaps.core == 0
    held = jnp.where(core, query, value) + swaps.swap_cores(jnp.where(core, value, query))
    halved = 0
    for stage in range(swaps.count()):
        rows = held.shape[0] // 2
        if stage == halved and rows % SUBLANES == 0:
            high = swaps.high(stage)
            low_half, high_half = held[:rows], held[rows:]
            sent = jnp.where(high, low_half, high_half)
            held = jnp.where(high, high_half, low_half) + swaps.swap(stage, sent)
            halved += 1
        else:
            held = held + swaps.swap(stage, held)
    held = held[:, :width] / held[:, width:width + 1]
    for stage in reversed(range(halved)):
        high = swaps.high(stage)
        other = swaps.swap(stage, held)
        held = jnp.concatenate([jnp.where(high, other, held), jnp.where(high, held, other)], axis=0)
    other = swaps.swap_cores(held)
    query = jnp.where(core, held, other)
    value = jnp.where(core, other, held)
    return query[:rank_dim], query[rank_dim:], value[:rank_dim], value[rank_dim:]


def solution(mesh):
    sizes = dict(mesh.shape)
    split = P(AXES)
    placed = (split, split, split, P(), P(), P(), P(), split)

    def step(*args):
        return body(sizes, *args)

    return jax.shard_map(step, mesh=mesh, in_specs=placed, out_specs=(P(),) * 4, check_vma=False)
```

```python
import functools

import jax
import jax.numpy as jnp
from jax import lax
from jax.experimental import pallas as pl
from jax.experimental.pallas import tpu as pltpu
from jax.sharding import PartitionSpec as P

AXES = ("gx", "gy", "gz")
LANES = 128
SUBLANES = 8
PARTS = 4
NT = (((1,), (1,)), ((), ()))
NN = (((1,), (0,)), ((), ()))
dot = functools.partial(lax.dot_general, preferred_element_type=jnp.float32)


def adapter_kernel(
    parts, flip, lengths_in, rows, query_grad, value_grad, query_down, value_down, query_up, value_up,
    down_sum, up_sum, held_rows, held_grad, held_down, held_up, lengths, sems,
):
    tokens, width = held_rows.shape
    step = width // parts
    cuts = [pl.ds(k * step, step) for k in range(parts)]
    query = ((lax.axis_index("gx") + flip) & 1) == 0

    def copies(down, up, grad):
        small = [
            pltpu.make_async_copy(down, held_down, sems.at[0, parts]),
            pltpu.make_async_copy(up, held_up, sems.at[1, parts]),
            pltpu.make_async_copy(lengths_in, lengths, sems.at[0, parts + 1]),
        ]
        large = [
            (
                pltpu.make_async_copy(rows.at[:, cut], held_rows.at[:, cut], sems.at[0, k]),
                pltpu.make_async_copy(grad.at[:, cut], held_grad.at[:, cut], sems.at[1, k]),
            )
            for k, cut in enumerate(cuts)
        ]
        return small, large

    def start(*which):
        small, large = copies(*which)
        for copy in small:
            copy.start()
        for pair in large:
            for copy in pair:
                copy.start()

    @pl.when(query)
    def _():
        start(query_down, query_up, query_grad)

    @pl.when(jnp.logical_not(query))
    def _():
        start(value_down, value_up, value_grad)

    small, large = copies(query_down, query_up, query_grad)
    for copy in small:
        copy.wait()
    inner = back = 0.0
    for cut, pair in zip(cuts, large):
        for copy in pair:
            copy.wait()
        inner = inner + dot(held_down[:, cut], held_rows[:, cut], NT)
        back = back + dot(held_up[:, cut], held_grad[:, cut], NT)
    seqs = lengths.shape[0]
    seq_len = tokens // seqs
    token = lax.broadcasted_iota(jnp.int32, inner.shape, 1)
    valid = token < 0
    count = 0
    for s in range(seqs):
        first = s * seq_len
        valid = valid | ((token >= first) & (token < first + lengths[s]))
        count = count + lengths[s]
    inner = jnp.where(valid, inner, 0.0).astype(jnp.bfloat16)
    back = jnp.where(valid, back, 0.0).astype(jnp.bfloat16)
    for cut in cuts:
        down_sum[:, cut] = dot(back, held_rows[:, cut], NN)
        up_sum[:, cut] = dot(inner, held_grad[:, cut], NN)
    down_sum[:, width:] = jnp.full((down_sum.shape[0], LANES), count.astype(jnp.float32), jnp.float32)


def adapter_sums(flip, lengths, rows, *rest):
    tokens, width = rows.shape
    rank = rest[-1].shape[0]
    wide = pltpu.VMEM((tokens, width), rows.dtype)
    thin = pltpu.VMEM((rank, width), rows.dtype)
    args = [pltpu.with_memory_space_constraint(x, pltpu.HBM) for x in (lengths, rows, *rest)]
    return pl.pallas_call(
        functools.partial(adapter_kernel, PARTS, flip),
        out_shape=(pltpu.VMEM((rank, width + LANES), jnp.float32), pltpu.VMEM((rank, width), jnp.float32)),
        in_specs=[pl.BlockSpec(memory_space=pltpu.HBM)] * len(args),
        out_specs=(pl.BlockSpec(memory_space=pltpu.VMEM),) * 2,
        scratch_shapes=[
            wide, wide, thin, thin, pltpu.SMEM(lengths.shape, lengths.dtype),
            pltpu.SemaphoreType.DMA((2, PARTS + 2)),
        ],
        compiler_params=pltpu.CompilerParams(vmem_limit_bytes=16 << 20),
        cost_estimate=pl.CostEstimate(
            flops=8 * rank * tokens * width, bytes_accessed=4 * tokens * width, transcendentals=0
        ),
        name="adapter",
    )(*args)


def axis_bits(axis, size, first=0):
    bits = size.bit_length() - 1
    assert size == 1 << bits
    return [(axis, 1 << k) for k in range(first, bits)]


class Swaps:
    def __init__(self, sizes):
        self.sizes = sizes
        near = axis_bits("gx", sizes["gx"], 1) + axis_bits("gy", sizes["gy"])
        far = axis_bits("gz", sizes["gz"])
        self.orders = (near + far, self.paired(near) + self.paired(far))
        self.at = {axis: lax.axis_index(axis) for axis in AXES}
        self.core = self.at["gx"] & 1

    @staticmethod
    def paired(bits):
        order = list(bits)
        for k in range(0, len(order) - 1, 2):
            order[k], order[k + 1] = order[k + 1], order[k]
        return order

    def count(self):
        return len(self.orders[0])

    def high(self, stage):
        flags = [(self.at[axis] & bit) != 0 for axis, bit in (order[stage] for order in self.orders)]
        return jnp.where(self.core == 0, flags[0], flags[1])

    def swap(self, stage, array):
        gx, gy, gz = (self.sizes[axis] for axis in AXES)
        pairs = []
        for i in range(gx):
            for j in range(gy):
                for k in range(gz):
                    place = {"gx": i, "gy": j, "gz": k}
                    axis, bit = self.orders[i & 1][stage]
                    place[axis] ^= bit
                    there = (place["gx"] * gy + place["gy"]) * gz + place["gz"]
                    pairs.append(((i * gy + j) * gz + k, there))
        return lax.ppermute(array, AXES, pairs)

    def swap_cores(self, array):
        return lax.ppermute(array, "gx", [(i, i ^ 1) for i in range(self.sizes["gx"])])


def halves(array, width, axis):
    if axis == 0:
        rows = array.shape[0] // 2
        return array[:rows], array[rows:]
    tail = array[:, width:]
    half = width // 2
    low, high = array[:, :half], array[:, half:width]
    if not tail.shape[1]:
        return low, high
    return jnp.concatenate([low, tail], axis=1), jnp.concatenate([high, tail], axis=1)


def body(sizes, hidden_rows, query_grad, value_grad, query_down, query_up, value_down, value_up, lengths):
    args = (lengths, hidden_rows, query_grad, value_grad, query_down, value_down, query_up, value_up)
    swaps = Swaps(sizes)
    widths = [hidden_rows.shape[1]] * 2
    sent = adapter_sums(1, *args)
    got = [swaps.swap_cores(x) for x in sent]
    kept = adapter_sums(0, *args)
    held = [x + y for x, y in zip(kept, got)]
    cut = []
    for stage in range(swaps.count()):
        axis = None
        if stage == len(cut):
            if held[0].shape[0] % (2 * SUBLANES) == 0:
                axis = 0
            elif widths[0] % (2 * LANES) == 0 and len(cut) < 2:
                axis = 1
        if axis is None:
            held = [x + swaps.swap(stage, x) for x in held]
            continue
        high = swaps.high(stage)
        for c, x in enumerate(held):
            low_half, high_half = halves(x, widths[c], axis)
            held[c] = jnp.where(high, high_half, low_half) + swaps.swap(stage, jnp.where(high, low_half, high_half))
            if axis == 1:
                widths[c] //= 2
        cut.append(axis)
    total = held[0][0, widths[0]]
    held = [x[:, :width] for x, width in zip(held, widths)]
    for stage, axis in reversed(list(enumerate(cut))):
        high = swaps.high(stage)
        for c, x in enumerate(held):
            other = swaps.swap(stage, x)
            held[c] = jnp.concatenate([jnp.where(high, other, x), jnp.where(high, x, other)], axis=axis)
    core = swaps.core == 0
    query, value = [], []
    for x in held:
        other = swaps.swap_cores(x)
        query.append(jnp.where(core, x, other) / total)
        value.append(jnp.where(core, other, x) / total)
    return (*query, *value)


def solution(mesh):
    sizes = dict(mesh.shape)
    split = P(AXES)
    placed = (split, split, split, P(), P(), P(), P(), split)

    def step(*args):
        return body(sizes, *args)

    return jax.shard_map(step, mesh=mesh, in_specs=placed, out_specs=(P(),) * 4, check_vma=False)
```

```python
import functools

import jax
import jax.numpy as jnp
from jax import lax
from jax.experimental import pallas as pl
from jax.experimental.pallas import tpu as pltpu
from jax.sharding import PartitionSpec as P

AXES = ("gx", "gy", "gz")
LANES = 128
SUBLANES = 8
PARTS = 4
NT = (((1,), (1,)), ((), ()))
NN = (((1,), (0,)), ((), ()))
dot = functools.partial(lax.dot_general, preferred_element_type=jnp.float32)


def adapter_kernel(
    parts, flip, lengths_in, rows, query_grad, value_grad, query_down, value_down, query_up, value_up,
    down_sum, up_sum, held_rows, held_grad, held_down, held_up, lengths, sems,
):
    tokens, width = held_rows.shape
    step = width // parts
    cuts = [pl.ds(k * step, step) for k in range(parts)]
    query = ((lax.axis_index("gx") + flip) & 1) == 0

    def copies(down, up, grad):
        small = [
            pltpu.make_async_copy(down, held_down, sems.at[0, parts]),
            pltpu.make_async_copy(up, held_up, sems.at[1, parts]),
            pltpu.make_async_copy(lengths_in, lengths, sems.at[0, parts + 1]),
        ]
        large = [
            (
                pltpu.make_async_copy(rows.at[:, cut], held_rows.at[:, cut], sems.at[0, k]),
                pltpu.make_async_copy(grad.at[:, cut], held_grad.at[:, cut], sems.at[1, k]),
            )
            for k, cut in enumerate(cuts)
        ]
        return small, large

    def start(*which):
        small, large = copies(*which)
        for copy in small:
            copy.start()
        for pair in large:
            for copy in pair:
                copy.start()

    @pl.when(query)
    def _():
        start(query_down, query_up, query_grad)

    @pl.when(jnp.logical_not(query))
    def _():
        start(value_down, value_up, value_grad)

    small, large = copies(query_down, query_up, query_grad)
    for copy in small:
        copy.wait()
    inner = back = 0.0
    for cut, pair in zip(cuts, large):
        for copy in pair:
            copy.wait()
        inner = inner + dot(held_down[:, cut], held_rows[:, cut], NT)
        back = back + dot(held_up[:, cut], held_grad[:, cut], NT)
    seqs = lengths.shape[0]
    seq_len = tokens // seqs
    token = lax.broadcasted_iota(jnp.int32, inner.shape, 1)
    valid = token < 0
    count = 0
    for s in range(seqs):
        first = s * seq_len
        valid = valid | ((token >= first) & (token < first + lengths[s]))
        count = count + lengths[s]
    inner = jnp.where(valid, inner, 0.0).astype(jnp.bfloat16)
    back = jnp.where(valid, back, 0.0).astype(jnp.bfloat16)
    for cut in cuts:
        down_sum[:, cut] = dot(back, held_rows[:, cut], NN)
        up_sum[:, cut] = dot(inner, held_grad[:, cut], NN)
    down_sum[:, width:] = jnp.full((down_sum.shape[0], LANES), count.astype(jnp.float32), jnp.float32)


def adapter_sums(flip, lengths, rows, *rest):
    tokens, width = rows.shape
    rank = rest[-1].shape[0]
    wide = pltpu.VMEM((tokens, width), rows.dtype)
    thin = pltpu.VMEM((rank, width), rows.dtype)
    args = [pltpu.with_memory_space_constraint(x, pltpu.HBM) for x in (lengths, rows, *rest)]
    return pl.pallas_call(
        functools.partial(adapter_kernel, PARTS, flip),
        out_shape=(pltpu.VMEM((rank, width + LANES), jnp.float32), pltpu.VMEM((rank, width), jnp.float32)),
        in_specs=[pl.BlockSpec(memory_space=pltpu.HBM)] * len(args),
        out_specs=(pl.BlockSpec(memory_space=pltpu.VMEM),) * 2,
        scratch_shapes=[
            wide, wide, thin, thin, pltpu.SMEM(lengths.shape, lengths.dtype),
            pltpu.SemaphoreType.DMA((2, PARTS + 2)),
        ],
        compiler_params=pltpu.CompilerParams(vmem_limit_bytes=16 << 20),
        cost_estimate=pl.CostEstimate(
            flops=8 * rank * tokens * width, bytes_accessed=4 * tokens * width, transcendentals=0
        ),
        name="adapter",
    )(*args)


def finish_kernel(mine, other, total, query, value, out, sems):
    core = lax.axis_index("gx") & 1
    rows = mine.shape[0] // 2
    by = total[0, 0]
    copies = []
    for k in range(2):
        cut = pl.ds(k * rows, rows)
        out[core, cut] = mine[cut] / by
        out[1 - core, cut] = other[cut] / by
        for c, target in enumerate((query, value)):
            copies.append(pltpu.make_async_copy(out.at[c, cut], target.at[cut], sems.at[c, k]))
            copies[-1].start()
    for copy in copies:
        copy.wait()


def finish(mine, other, total):
    near = pl.BlockSpec(memory_space=pltpu.VMEM)
    far = pl.BlockSpec(memory_space=pltpu.HBM)
    return pl.pallas_call(
        finish_kernel,
        out_shape=(jax.ShapeDtypeStruct(mine.shape, mine.dtype),) * 2,
        in_specs=[near] * 3,
        out_specs=(far,) * 2,
        scratch_shapes=[pltpu.VMEM((2, *mine.shape), mine.dtype), pltpu.SemaphoreType.DMA((2, 2))],
        compiler_params=pltpu.CompilerParams(vmem_limit_bytes=8 << 20),
        cost_estimate=pl.CostEstimate(flops=2 * mine.size, bytes_accessed=16 * mine.size, transcendentals=0),
        name="finish",
    )(*(pltpu.with_memory_space_constraint(x, pltpu.VMEM) for x in (mine, other, total)))


def axis_bits(axis, size, first=0):
    bits = size.bit_length() - 1
    assert size == 1 << bits
    return [(axis, 1 << k) for k in range(first, bits)]


class Swaps:
    def __init__(self, sizes):
        self.sizes = sizes
        near = axis_bits("gx", sizes["gx"], 1) + axis_bits("gy", sizes["gy"])
        far = axis_bits("gz", sizes["gz"])
        self.orders = (near + far, self.paired(near) + self.paired(far))
        self.at = {axis: lax.axis_index(axis) for axis in AXES}
        self.core = self.at["gx"] & 1

    @staticmethod
    def paired(bits):
        order = list(bits)
        for k in range(0, len(order) - 1, 2):
            order[k], order[k + 1] = order[k + 1], order[k]
        return order

    def count(self):
        return len(self.orders[0])

    def high(self, stage, chain):
        flags = [(self.at[axis] & bit) != 0 for axis, bit in (order[stage] for order in self.orders)]
        return jnp.where(self.core == chain, flags[0], flags[1])

    def swap(self, stage, chain, array):
        gx, gy, gz = (self.sizes[axis] for axis in AXES)
        pairs = []
        for i in range(gx):
            for j in range(gy):
                for k in range(gz):
                    place = {"gx": i, "gy": j, "gz": k}
                    axis, bit = self.orders[(i & 1) ^ chain][stage]
                    place[axis] ^= bit
                    there = (place["gx"] * gy + place["gy"]) * gz + place["gz"]
                    pairs.append(((i * gy + j) * gz + k, there))
        return lax.ppermute(array, AXES, pairs)

    def swap_cores(self, array):
        return lax.ppermute(array, "gx", [(i, i ^ 1) for i in range(self.sizes["gx"])])


def halves(array, width, axis):
    if axis == 0:
        rows = array.shape[0] // 2
        return array[:rows], array[rows:]
    tail = array[:, width:]
    half = width // 2
    low, high = array[:, :half], array[:, half:width]
    if not tail.shape[1]:
        return low, high
    return jnp.concatenate([low, tail], axis=1), jnp.concatenate([high, tail], axis=1)


def body(sizes, hidden_rows, query_grad, value_grad, query_down, query_up, value_down, value_up, lengths):
    args = (lengths, hidden_rows, query_grad, value_grad, query_down, value_down, query_up, value_up)
    swaps = Swaps(sizes)
    widths = [hidden_rows.shape[1]] * 2
    sent = adapter_sums(1, *args)
    got = [swaps.swap_cores(x) for x in sent]
    kept = adapter_sums(0, *args)
    held = [x + y for x, y in zip(kept, got)]
    cut = []
    for stage in range(swaps.count()):
        axis = None
        if stage == len(cut):
            if held[0].shape[0] % (2 * SUBLANES) == 0:
                axis = 0
            elif widths[0] % (2 * LANES) == 0 and len(cut) < 2:
                axis = 1
        if axis is None:
            held = [x + swaps.swap(stage, c, x) for c, x in enumerate(held)]
            continue
        for c, x in enumerate(held):
            high = swaps.high(stage, c)
            low_half, high_half = halves(x, widths[c], axis)
            sent = jnp.where(high, low_half, high_half)
            held[c] = jnp.where(high, high_half, low_half) + swaps.swap(stage, c, sent)
            if axis == 1:
                widths[c] //= 2
        cut.append(axis)
    total = held[0][:, widths[0]:]
    held = [x[:, :width] for x, width in zip(held, widths)]
    for stage, axis in reversed(list(enumerate(cut))):
        for c, x in enumerate(held):
            high = swaps.high(stage, c)
            other = swaps.swap(stage, c, x)
            held[c] = jnp.concatenate([jnp.where(high, other, x), jnp.where(high, x, other)], axis=axis)
    query, value = zip(*(finish(x, swaps.swap_cores(x), total) for x in held))
    return (*query, *value)


def solution(mesh):
    sizes = dict(mesh.shape)
    split = P(AXES)
    placed = (split, split, split, P(), P(), P(), P(), split)

    def step(*args):
        return body(sizes, *args)

    return jax.shard_map(step, mesh=mesh, in_specs=placed, out_specs=(P(),) * 4, check_vma=False)
```

```python
import functools

import jax
import jax.numpy as jnp
from jax import lax
from jax.experimental import pallas as pl
from jax.experimental.pallas import tpu as pltpu
from jax.sharding import PartitionSpec as P

AXES = ("gx", "gy", "gz")
LANES = 128
SUBLANES = 8
PARTS = 4
NT = (((1,), (1,)), ((), ()))
NN = (((1,), (0,)), ((), ()))
dot = functools.partial(lax.dot_general, preferred_element_type=jnp.float32)


def role_of(gx, gy, gz):
    return (gx ^ (gx >> 1) ^ gy ^ gz) & 1


def role_here():
    return role_of(*(lax.axis_index(axis) for axis in AXES))


def adapter_kernel(
    parts, flip, lengths_in, rows, query_grad, value_grad, query_down, value_down, query_up, value_up,
    down_sum, up_sum, held_rows, held_grad, held_down, held_up, lengths, sems,
):
    tokens, width = held_rows.shape
    step = width // parts
    cuts = [pl.ds(k * step, step) for k in range(parts)]
    query = (role_here() ^ flip) == 0

    def copies(down, up, grad):
        small = [
            pltpu.make_async_copy(down, held_down, sems.at[0, parts]),
            pltpu.make_async_copy(up, held_up, sems.at[1, parts]),
            pltpu.make_async_copy(lengths_in, lengths, sems.at[0, parts + 1]),
        ]
        large = [
            (
                pltpu.make_async_copy(rows.at[:, cut], held_rows.at[:, cut], sems.at[0, k]),
                pltpu.make_async_copy(grad.at[:, cut], held_grad.at[:, cut], sems.at[1, k]),
            )
            for k, cut in enumerate(cuts)
        ]
        return small, large

    def start(*which):
        small, large = copies(*which)
        for copy in small:
            copy.start()
        for pair in large:
            for copy in pair:
                copy.start()

    @pl.when(query)
    def _():
        start(query_down, query_up, query_grad)

    @pl.when(jnp.logical_not(query))
    def _():
        start(value_down, value_up, value_grad)

    small, large = copies(query_down, query_up, query_grad)
    for copy in small:
        copy.wait()
    inner = back = 0.0
    for cut, pair in zip(cuts, large):
        for copy in pair:
            copy.wait()
        inner = inner + dot(held_down[:, cut], held_rows[:, cut], NT)
        back = back + dot(held_up[:, cut], held_grad[:, cut], NT)
    seqs = lengths.shape[0]
    seq_len = tokens // seqs
    token = lax.broadcasted_iota(jnp.int32, inner.shape, 1)
    valid = token < 0
    count = 0
    for s in range(seqs):
        first = s * seq_len
        valid = valid | ((token >= first) & (token < first + lengths[s]))
        count = count + lengths[s]
    inner = jnp.where(valid, inner, 0.0).astype(jnp.bfloat16)
    back = jnp.where(valid, back, 0.0).astype(jnp.bfloat16)
    for cut in cuts:
        down_sum[:, cut] = dot(back, held_rows[:, cut], NN)
        up_sum[:, cut] = dot(inner, held_grad[:, cut], NN)
    down_sum[:, width:] = jnp.full((down_sum.shape[0], LANES), count.astype(jnp.float32), jnp.float32)


def adapter_sums(flip, lengths, rows, *rest):
    tokens, width = rows.shape
    rank = rest[-1].shape[0]
    wide = pltpu.VMEM((tokens, width), rows.dtype)
    thin = pltpu.VMEM((rank, width), rows.dtype)
    args = [pltpu.with_memory_space_constraint(x, pltpu.HBM) for x in (lengths, rows, *rest)]
    return pl.pallas_call(
        functools.partial(adapter_kernel, PARTS, flip),
        out_shape=(pltpu.VMEM((rank, width + LANES), jnp.float32), pltpu.VMEM((rank, width), jnp.float32)),
        in_specs=[pl.BlockSpec(memory_space=pltpu.HBM)] * len(args),
        out_specs=(pl.BlockSpec(memory_space=pltpu.VMEM),) * 2,
        scratch_shapes=[
            wide, wide, thin, thin, pltpu.SMEM(lengths.shape, lengths.dtype),
            pltpu.SemaphoreType.DMA((2, PARTS + 2)),
        ],
        compiler_params=pltpu.CompilerParams(vmem_limit_bytes=16 << 20),
        cost_estimate=pl.CostEstimate(
            flops=8 * rank * tokens * width, bytes_accessed=4 * tokens * width, transcendentals=0
        ),
        name="adapter",
    )(*args)


def finish_kernel(mine, other, total, query, value, out, sems):
    role = role_here()
    rows = mine.shape[0] // 2
    by = total[0, 0]
    copies = []
    for k in range(2):
        cut = pl.ds(k * rows, rows)
        out[role, cut] = mine[cut] / by
        out[1 - role, cut] = other[cut] / by
        for c, target in enumerate((query, value)):
            copies.append(pltpu.make_async_copy(out.at[c, cut], target.at[cut], sems.at[c, k]))
            copies[-1].start()
    for copy in copies:
        copy.wait()


def finish(mine, other, total):
    near = pl.BlockSpec(memory_space=pltpu.VMEM)
    far = pl.BlockSpec(memory_space=pltpu.HBM)
    return pl.pallas_call(
        finish_kernel,
        out_shape=(jax.ShapeDtypeStruct(mine.shape, mine.dtype),) * 2,
        in_specs=[near] * 3,
        out_specs=(far,) * 2,
        scratch_shapes=[pltpu.VMEM((2, *mine.shape), mine.dtype), pltpu.SemaphoreType.DMA((2, 2))],
        compiler_params=pltpu.CompilerParams(vmem_limit_bytes=8 << 20),
        cost_estimate=pl.CostEstimate(flops=2 * mine.size, bytes_accessed=16 * mine.size, transcendentals=0),
        name="finish",
    )(*(pltpu.with_memory_space_constraint(x, pltpu.VMEM) for x in (mine, other, total)))


def axis_bits(axis, size, first=0):
    bits = size.bit_length() - 1
    assert size == 1 << bits
    return [(axis, 1 << k) for k in range(first, bits)]


class Swaps:
    def __init__(self, sizes):
        self.sizes = sizes
        near = axis_bits("gx", sizes["gx"], 1) + axis_bits("gy", sizes["gy"])
        far = axis_bits("gz", sizes["gz"])
        self.orders = (near + far, self.paired(near) + self.paired(far))

    @staticmethod
    def paired(bits):
        order = list(bits)
        for k in range(0, len(order) - 1, 2):
            order[k], order[k + 1] = order[k + 1], order[k]
        return order

    def count(self):
        return len(self.orders[0])

    def high(self, stage):
        flags = [(lax.axis_index(axis) & bit) != 0 for axis, bit in (order[stage] for order in self.orders)]
        return jnp.where(role_here() == 0, flags[0], flags[1])

    def swap(self, stage, array):
        gx, gy, gz = (self.sizes[axis] for axis in AXES)
        pairs = []
        for i in range(gx):
            for j in range(gy):
                for k in range(gz):
                    role = role_of(i, j, k)
                    place = {"gx": i, "gy": j, "gz": k}
                    axis, bit = self.orders[role][stage]
                    place[axis] ^= bit
                    place["gx"] ^= role_of(**place) ^ role
                    there = (place["gx"] * gy + place["gy"]) * gz + place["gz"]
                    pairs.append(((i * gy + j) * gz + k, there))
        return lax.ppermute(array, AXES, pairs)

    def swap_cores(self, array):
        return lax.ppermute(array, "gx", [(i, i ^ 1) for i in range(self.sizes["gx"])])


def halves(array, width, axis):
    if axis == 0:
        rows = array.shape[0] // 2
        return array[:rows], array[rows:]
    tail = array[:, width:]
    half = width // 2
    low, high = array[:, :half], array[:, half:width]
    if not tail.shape[1]:
        return low, high
    return jnp.concatenate([low, tail], axis=1), jnp.concatenate([high, tail], axis=1)


def body(sizes, hidden_rows, query_grad, value_grad, query_down, query_up, value_down, value_up, lengths):
    args = (lengths, hidden_rows, query_grad, value_grad, query_down, value_down, query_up, value_up)
    swaps = Swaps(sizes)
    widths = [hidden_rows.shape[1]] * 2
    sent = adapter_sums(1, *args)
    got = [swaps.swap_cores(x) for x in sent]
    kept = adapter_sums(0, *args)
    held = [x + y for x, y in zip(kept, got)]
    cut = []
    for stage in range(swaps.count()):
        axis = None
        if stage == len(cut):
            if held[0].shape[0] % (2 * SUBLANES) == 0:
                axis = 0
            elif widths[0] % (2 * LANES) == 0 and len(cut) < 2:
                axis = 1
        if axis is None:
            held = [x + swaps.swap(stage, x) for x in held]
            continue
        high = swaps.high(stage)
        for c, x in enumerate(held):
            low_half, high_half = halves(x, widths[c], axis)
            sent = jnp.where(high, low_half, high_half)
            held[c] = jnp.where(high, high_half, low_half) + swaps.swap(stage, sent)
            if axis == 1:
                widths[c] //= 2
        cut.append(axis)
    total = held[0][:, widths[0]:]
    held = [x[:, :width] for x, width in zip(held, widths)]
    for stage, axis in reversed(list(enumerate(cut))):
        high = swaps.high(stage)
        for c, x in enumerate(held):
            other = swaps.swap(stage, x)
            held[c] = jnp.concatenate([jnp.where(high, other, x), jnp.where(high, x, other)], axis=axis)
    query, value = zip(*(finish(x, swaps.swap_cores(x), total) for x in held))
    return (*query, *value)


def solution(mesh):
    sizes = dict(mesh.shape)
    split = P(AXES)
    placed = (split, split, split, P(), P(), P(), P(), split)

    def step(*args):
        return body(sizes, *args)

    return jax.shard_map(step, mesh=mesh, in_specs=placed, out_specs=(P(),) * 4, check_vma=False)
```

```python
import functools

import jax
import jax.numpy as jnp
from jax import lax
from jax.experimental import pallas as pl
from jax.experimental.pallas import tpu as pltpu
from jax.sharding import PartitionSpec as P

AXES = ("gx", "gy", "gz")
LANES = 128
SUBLANES = 8
PARTS = 4
NT = (((1,), (1,)), ((), ()))
NN = (((1,), (0,)), ((), ()))
dot = functools.partial(lax.dot_general, preferred_element_type=jnp.float32)


def role_of(gx, gy, gz):
    return (gx ^ (gx >> 1) ^ gy ^ gz) & 1


def role_here():
    return role_of(*(lax.axis_index(axis) for axis in AXES))


def store_sums(lengths, rows, grad, down, up, down_sum, up_sum, arrive, rows_held):
    tokens, width = rows.shape
    step = width // PARTS
    cuts = [pl.ds(k * step, step) for k in range(PARTS)]
    inner = back = 0.0
    order = [("rows", k) for k in range(PARTS)] + [("grad", k) for k in range(PARTS)]
    if not rows_held:
        order.sort(key=lambda item: item[1])
    for name, k in order:
        arrive(name, k)
        if name == "rows":
            inner = inner + dot(down[:, cuts[k]], rows[:, cuts[k]], NT)
        else:
            back = back + dot(up[:, cuts[k]], grad[:, cuts[k]], NT)
    arrive("lengths", 0)
    seqs = lengths.shape[0]
    seq_len = tokens // seqs
    token = lax.broadcasted_iota(jnp.int32, inner.shape, 1)
    valid = token < 0
    count = 0
    for s in range(seqs):
        first = s * seq_len
        valid = valid | ((token >= first) & (token < first + lengths[s]))
        count = count + lengths[s]
    inner = jnp.where(valid, inner, 0.0).astype(jnp.bfloat16)
    back = jnp.where(valid, back, 0.0).astype(jnp.bfloat16)
    for cut in cuts:
        down_sum[:, cut] = dot(back, rows[:, cut], NN)
        up_sum[:, cut] = dot(inner, grad[:, cut], NN)
    down_sum[:, width:] = jnp.full((down_sum.shape[0], LANES), count.astype(jnp.float32), jnp.float32)


def load_and_sum(flip, lengths_in, rows_in, queries, values, rows, held, lengths, down_sum, up_sum, sems):
    held_grad, held_down, held_up = held
    step = rows.shape[1] // PARTS

    def copies(which):
        grad, down, up = which
        plan = {
            ("maps", 0): pltpu.make_async_copy(down, held_down, sems.at[0, PARTS]),
            ("maps", 1): pltpu.make_async_copy(up, held_up, sems.at[1, PARTS]),
            ("lengths", 0): pltpu.make_async_copy(lengths_in, lengths, sems.at[0, PARTS + 1]),
        }
        for k in range(PARTS):
            cut = pl.ds(k * step, step)
            if rows_in is not None:
                plan["rows", k] = pltpu.make_async_copy(rows_in.at[:, cut], rows.at[:, cut], sems.at[0, k])
            plan["grad", k] = pltpu.make_async_copy(grad.at[:, cut], held_grad.at[:, cut], sems.at[1, k])
        return plan

    def start(which):
        for copy in copies(which).values():
            copy.start()

    query = (role_here() ^ flip) == 0
    pl.when(query)(lambda: start(queries))
    pl.when(jnp.logical_not(query))(lambda: start(values))
    plan = copies(queries)

    def arrive(*key):
        if key == ("rows", 0):
            plan["maps", 0].wait()
        if key == ("grad", 0):
            plan["maps", 1].wait()
        if key in plan:
            plan[key].wait()

    store_sums(lengths, rows, held_grad, held_down, held_up, down_sum, up_sum, arrive, rows_in is None)


def sent_kernel(
    lengths_in, rows_in, query_grad, value_grad, query_down, value_down, query_up, value_up,
    down_sum, up_sum, rows, held_grad, held_down, held_up, lengths, sems,
):
    queries, values = (query_grad, query_down, query_up), (value_grad, value_down, value_up)
    held = (held_grad, held_down, held_up)
    load_and_sum(1, lengths_in, rows_in, queries, values, rows, held, lengths, down_sum, up_sum, sems)


def kept_kernel(
    lengths_in, rows, query_grad, value_grad, query_down, value_down, query_up, value_up,
    down_sum, up_sum, held_grad, held_down, held_up, lengths, sems,
):
    queries, values = (query_grad, query_down, query_up), (value_grad, value_down, value_up)
    held = (held_grad, held_down, held_up)
    load_and_sum(0, lengths_in, None, queries, values, rows, held, lengths, down_sum, up_sum, sems)


def adapter_sums(lengths, rows, *rest):
    tokens, width = rows.shape
    rank = rest[-1].shape[0]
    wide = pltpu.VMEM((tokens, width), rows.dtype)
    thin = pltpu.VMEM((rank, width), rows.dtype)
    sums = (pltpu.VMEM((rank, width + LANES), jnp.float32), pltpu.VMEM((rank, width), jnp.float32))
    far, near = (pl.BlockSpec(memory_space=space) for space in (pltpu.HBM, pltpu.VMEM))
    common = dict(
        scratch_shapes=[
            wide, thin, thin, pltpu.SMEM(lengths.shape, lengths.dtype), pltpu.SemaphoreType.DMA((2, PARTS + 2))
        ],
        compiler_params=pltpu.CompilerParams(vmem_limit_bytes=16 << 20),
        cost_estimate=pl.CostEstimate(
            flops=8 * rank * tokens * width, bytes_accessed=4 * tokens * width, transcendentals=0
        ),
    )

    def put(space, *arrays):
        return [pltpu.with_memory_space_constraint(x, space) for x in arrays]

    first, *others = put(pltpu.HBM, lengths, *rest)
    *sent, held = pl.pallas_call(
        sent_kernel,
        out_shape=(*sums, wide),
        in_specs=[far] * (2 + len(others)),
        out_specs=(near,) * 3,
        name="sent",
        **common,
    )(first, *put(pltpu.HBM, rows), *others)

    def kept():
        return pl.pallas_call(
            kept_kernel,
            out_shape=sums,
            in_specs=[far, near] + [far] * len(others),
            out_specs=(near,) * 2,
            name="kept",
            **common,
        )(first, *put(pltpu.VMEM, held), *others)

    return sent, kept


def finish_kernel(mine, other, total, query, value, out, sems):
    role = role_here()
    rows = mine.shape[0] // 2
    by = total[0, 0]
    copies = []
    for k in range(2):
        cut = pl.ds(k * rows, rows)
        out[role, cut] = mine[cut] / by
        out[1 - role, cut] = other[cut] / by
        for c, target in enumerate((query, value)):
            copies.append(pltpu.make_async_copy(out.at[c, cut], target.at[cut], sems.at[c, k]))
            copies[-1].start()
    for copy in copies:
        copy.wait()


def finish(mine, other, total):
    near = pl.BlockSpec(memory_space=pltpu.VMEM)
    far = pl.BlockSpec(memory_space=pltpu.HBM)
    return pl.pallas_call(
        finish_kernel,
        out_shape=(jax.ShapeDtypeStruct(mine.shape, mine.dtype),) * 2,
        in_specs=[near] * 3,
        out_specs=(far,) * 2,
        scratch_shapes=[pltpu.VMEM((2, *mine.shape), mine.dtype), pltpu.SemaphoreType.DMA((2, 2))],
        compiler_params=pltpu.CompilerParams(vmem_limit_bytes=8 << 20),
        cost_estimate=pl.CostEstimate(flops=2 * mine.size, bytes_accessed=16 * mine.size, transcendentals=0),
        name="finish",
    )(*(pltpu.with_memory_space_constraint(x, pltpu.VMEM) for x in (mine, other, total)))


def axis_bits(axis, size, first=0):
    bits = size.bit_length() - 1
    assert size == 1 << bits
    return [(axis, 1 << k) for k in range(first, bits)]


class Swaps:
    def __init__(self, sizes):
        self.sizes = sizes
        near = axis_bits("gx", sizes["gx"], 1) + axis_bits("gy", sizes["gy"])
        far = axis_bits("gz", sizes["gz"])
        self.orders = (near + far, self.paired(near) + self.paired(far))

    @staticmethod
    def paired(bits):
        order = list(bits)
        for k in range(0, len(order) - 1, 2):
            order[k], order[k + 1] = order[k + 1], order[k]
        return order

    def count(self):
        return len(self.orders[0])

    def high(self, stage):
        flags = [(lax.axis_index(axis) & bit) != 0 for axis, bit in (order[stage] for order in self.orders)]
        return jnp.where(role_here() == 0, flags[0], flags[1])

    def swap(self, stage, array):
        gx, gy, gz = (self.sizes[axis] for axis in AXES)
        pairs = []
        for i in range(gx):
            for j in range(gy):
                for k in range(gz):
                    role = role_of(i, j, k)
                    place = {"gx": i, "gy": j, "gz": k}
                    axis, bit = self.orders[role][stage]
                    place[axis] ^= bit
                    place["gx"] ^= role_of(**place) ^ role
                    there = (place["gx"] * gy + place["gy"]) * gz + place["gz"]
                    pairs.append(((i * gy + j) * gz + k, there))
        return lax.ppermute(array, AXES, pairs)

    def swap_cores(self, array):
        return lax.ppermute(array, "gx", [(i, i ^ 1) for i in range(self.sizes["gx"])])


def halves(array, width, axis):
    if axis == 0:
        rows = array.shape[0] // 2
        return array[:rows], array[rows:]
    tail = array[:, width:]
    half = width // 2
    low, high = array[:, :half], array[:, half:width]
    if not tail.shape[1]:
        return low, high
    return jnp.concatenate([low, tail], axis=1), jnp.concatenate([high, tail], axis=1)


def body(sizes, hidden_rows, query_grad, value_grad, query_down, query_up, value_down, value_up, lengths):
    args = (lengths, hidden_rows, query_grad, value_grad, query_down, value_down, query_up, value_up)
    swaps = Swaps(sizes)
    widths = [hidden_rows.shape[1]] * 2
    sent, kept = adapter_sums(*args)
    got = [swaps.swap_cores(x) for x in sent]
    held = [x + y for x, y in zip(kept(), got)]
    cut = []
    for stage in range(swaps.count()):
        axis = None
        if stage == len(cut):
            if held[0].shape[0] % (2 * SUBLANES) == 0:
                axis = 0
            elif widths[0] % (2 * LANES) == 0 and len(cut) < 2:
                axis = 1
        if axis is None:
            held = [x + swaps.swap(stage, x) for x in held]
            continue
        high = swaps.high(stage)
        for c, x in enumerate(held):
            low_half, high_half = halves(x, widths[c], axis)
            sent = jnp.where(high, low_half, high_half)
            held[c] = jnp.where(high, high_half, low_half) + swaps.swap(stage, sent)
            if axis == 1:
                widths[c] //= 2
        cut.append(axis)
    total = held[0][:, widths[0]:]
    held = [x[:, :width] for x, width in zip(held, widths)]
    for stage, axis in reversed(list(enumerate(cut))):
        high = swaps.high(stage)
        for c, x in enumerate(held):
            other = swaps.swap(stage, x)
            held[c] = jnp.concatenate([jnp.where(high, other, x), jnp.where(high, x, other)], axis=axis)
    query, value = zip(*(finish(x, swaps.swap_cores(x), total) for x in held))
    return (*query, *value)


def solution(mesh):
    sizes = dict(mesh.shape)
    split = P(AXES)
    placed = (split, split, split, P(), P(), P(), P(), split)

    def step(*args):
        return body(sizes, *args)

    return jax.shard_map(step, mesh=mesh, in_specs=placed, out_specs=(P(),) * 4, check_vma=False)
```

```python
import functools

import jax
import jax.numpy as jnp
from jax import lax
from jax.experimental import pallas as pl
from jax.experimental.pallas import tpu as pltpu
from jax.sharding import PartitionSpec as P

AXES = ("gx", "gy", "gz")
LANES = 128
SUBLANES = 8
PARTS = 4
CHUNKS = 3
NT = (((1,), (1,)), ((), ()))
NN = (((1,), (0,)), ((), ()))
dot = functools.partial(lax.dot_general, preferred_element_type=jnp.float32)


def chunks_of(width):
    tiles = width // LANES
    ends = [-(-tiles * k // CHUNKS) * LANES for k in range(CHUNKS + 1)]
    return [(a, b - a) for a, b in zip(ends, ends[1:])]


def role_of(gx, gy, gz):
    bits = gx ^ gy ^ gz
    for shift in (8, 4, 2, 1):
        bits = bits ^ (bits >> shift)
    return bits & 1


def role_here():
    return role_of(*(lax.axis_index(axis) for axis in AXES))


def adapter_kernel(
    parts, flip, lengths_in, rows, query_grad, value_grad, query_down, value_down, query_up, value_up,
    *refs,
):
    *sums, held_rows, held_grad, held_down, held_up, lengths, sems = refs
    tokens, width = held_rows.shape
    step = width // parts
    cuts = [pl.ds(k * step, step) for k in range(parts)]
    query = (role_here() ^ flip) == 0

    def copies(down, up, grad):
        small = [
            pltpu.make_async_copy(down, held_down, sems.at[0, parts]),
            pltpu.make_async_copy(up, held_up, sems.at[1, parts]),
            pltpu.make_async_copy(lengths_in, lengths, sems.at[0, parts + 1]),
        ]
        large = [
            (
                pltpu.make_async_copy(rows.at[:, cut], held_rows.at[:, cut], sems.at[0, k]),
                pltpu.make_async_copy(grad.at[:, cut], held_grad.at[:, cut], sems.at[1, k]),
            )
            for k, cut in enumerate(cuts)
        ]
        return small, large

    def start(*which):
        small, large = copies(*which)
        for copy in small:
            copy.start()
        for pair in large:
            for copy in pair:
                copy.start()

    @pl.when(query)
    def _():
        start(query_down, query_up, query_grad)

    @pl.when(jnp.logical_not(query))
    def _():
        start(value_down, value_up, value_grad)

    small, large = copies(query_down, query_up, query_grad)
    for copy in small:
        copy.wait()
    inner = back = 0.0
    for cut, pair in zip(cuts, large):
        for copy in pair:
            copy.wait()
        inner = inner + dot(held_down[:, cut], held_rows[:, cut], NT)
        back = back + dot(held_up[:, cut], held_grad[:, cut], NT)
    seqs = lengths.shape[0]
    seq_len = tokens // seqs
    token = lax.broadcasted_iota(jnp.int32, inner.shape, 1)
    valid = token < 0
    count = 0
    for s in range(seqs):
        first = s * seq_len
        valid = valid | ((token >= first) & (token < first + lengths[s]))
        count = count + lengths[s]
    inner = jnp.where(valid, inner, 0.0).astype(jnp.bfloat16)
    back = jnp.where(valid, back, 0.0).astype(jnp.bfloat16)
    rank = inner.shape[0]
    for block, (first, columns) in zip(sums, chunks_of(width)):
        cut = pl.ds(first, columns)
        block[:rank, :columns] = dot(back, held_rows[:, cut], NN)
        block[rank:, :columns] = dot(inner, held_grad[:, cut], NN)
    sums[-1][:, columns:] = jnp.full((2 * rank, LANES), count.astype(jnp.float32), jnp.float32)


def adapter_sums(flip, lengths, rows, *rest):
    tokens, width = rows.shape
    rank = rest[-1].shape[0]
    wide = pltpu.VMEM((tokens, width), rows.dtype)
    thin = pltpu.VMEM((rank, width), rows.dtype)
    widths = [columns for _, columns in chunks_of(width)]
    widths[-1] += LANES
    args = [pltpu.with_memory_space_constraint(x, pltpu.HBM) for x in (lengths, rows, *rest)]
    return pl.pallas_call(
        functools.partial(adapter_kernel, PARTS, flip),
        out_shape=tuple(pltpu.VMEM((2 * rank, columns), jnp.float32) for columns in widths),
        in_specs=[pl.BlockSpec(memory_space=pltpu.HBM)] * len(args),
        out_specs=(pl.BlockSpec(memory_space=pltpu.VMEM),) * len(widths),
        scratch_shapes=[
            wide, wide, thin, thin, pltpu.SMEM(lengths.shape, lengths.dtype),
            pltpu.SemaphoreType.DMA((2, PARTS + 2)),
        ],
        compiler_params=pltpu.CompilerParams(vmem_limit_bytes=16 << 20),
        cost_estimate=pl.CostEstimate(
            flops=8 * rank * tokens * width, bytes_accessed=4 * tokens * width, transcendentals=0
        ),
        name="adapter",
    )(*args)


def finish_kernel(first, mine, other, total, *refs):
    *targets, out, sems = refs[-6:]
    role = role_here()
    rank = mine.shape[0] // 2
    columns = pl.ds(first, mine.shape[1])
    by = total[0, 0]
    copies = []
    for k in range(2):
        cut = pl.ds(k * rank, rank)
        out[role, cut] = mine[cut] / by
        out[1 - role, cut] = other[cut] / by
        for c in range(2):
            target = targets[2 * c + k].at[:, columns]
            copies.append(pltpu.make_async_copy(out.at[c, cut], target, sems.at[c, k]))
            copies[-1].start()
    for copy in copies:
        copy.wait()


def finish(first, width, mine, other, total, outs):
    near = pl.BlockSpec(memory_space=pltpu.VMEM)
    far = pl.BlockSpec(memory_space=pltpu.HBM)
    shape = (mine.shape[0] // 2, width)
    return pl.pallas_call(
        functools.partial(finish_kernel, first),
        out_shape=(jax.ShapeDtypeStruct(shape, mine.dtype),) * 4,
        in_specs=[near] * 3 + [far] * len(outs),
        out_specs=(far,) * 4,
        scratch_shapes=[pltpu.VMEM((2, *mine.shape), mine.dtype), pltpu.SemaphoreType.DMA((2, 2))],
        input_output_aliases={3 + k: k for k in range(len(outs))},
        compiler_params=pltpu.CompilerParams(vmem_limit_bytes=8 << 20),
        cost_estimate=pl.CostEstimate(flops=2 * mine.size, bytes_accessed=16 * mine.size, transcendentals=0),
        name="finish",
    )(*(pltpu.with_memory_space_constraint(x, pltpu.VMEM) for x in (mine, other, total)), *outs)


def axis_bits(axis, size, first=0):
    bits = size.bit_length() - 1
    assert size == 1 << bits
    return [(axis, 1 << k) for k in range(first, bits)]


class Swaps:
    def __init__(self, sizes):
        self.sizes = sizes
        near = axis_bits("gx", sizes["gx"], 1) + axis_bits("gy", sizes["gy"])
        far = axis_bits("gz", sizes["gz"])
        self.orders = (near + far, self.paired(near) + self.paired(far))

    @staticmethod
    def paired(bits):
        order = list(bits)
        for k in range(0, len(order) - 1, 2):
            order[k], order[k + 1] = order[k + 1], order[k]
        return order

    def count(self):
        return len(self.orders[0])

    def high(self, stage):
        flags = [(lax.axis_index(axis) & bit) != 0 for axis, bit in (order[stage] for order in self.orders)]
        return jnp.where(role_here() == 0, flags[0], flags[1])

    def swap(self, stage, array):
        gx, gy, gz = (self.sizes[axis] for axis in AXES)
        pairs = []
        for i in range(gx):
            for j in range(gy):
                for k in range(gz):
                    role = role_of(i, j, k)
                    place = {"gx": i, "gy": j, "gz": k}
                    axis, bit = self.orders[role][stage]
                    place[axis] ^= bit
                    place["gx"] ^= role_of(**place) ^ role
                    there = (place["gx"] * gy + place["gy"]) * gz + place["gz"]
                    pairs.append(((i * gy + j) * gz + k, there))
        return lax.ppermute(array, AXES, pairs)

    def swap_cores(self, array):
        return lax.ppermute(array, "gx", [(i, i ^ 1) for i in range(self.sizes["gx"])])


def body(sizes, hidden_rows, query_grad, value_grad, query_down, query_up, value_down, value_up, lengths):
    args = (lengths, hidden_rows, query_grad, value_grad, query_down, value_down, query_up, value_up)
    swaps = Swaps(sizes)
    sent = adapter_sums(1, *args)
    got = [swaps.swap_cores(x) for x in sent]
    kept = adapter_sums(0, *args)
    held = [x + y for x, y in zip(kept, got)]
    halved = 0
    for stage in range(swaps.count()):
        rows = held[0].shape[0] // 2
        if stage > halved or rows % SUBLANES:
            held = [x + swaps.swap(stage, x) for x in held]
            continue
        high = swaps.high(stage)
        for c, x in enumerate(held):
            sent = jnp.where(high, x[:rows], x[rows:])
            held[c] = jnp.where(high, x[rows:], x[:rows]) + swaps.swap(stage, sent)
        halved += 1
    width = hidden_rows.shape[1]
    blocks = chunks_of(width)
    total = held[-1][:, blocks[-1][1]:]
    held[-1] = held[-1][:, :blocks[-1][1]]
    for stage in reversed(range(halved)):
        high = swaps.high(stage)
        for c, x in enumerate(held):
            other = swaps.swap(stage, x)
            held[c] = jnp.concatenate([jnp.where(high, other, x), jnp.where(high, x, other)], axis=0)
    outs = ()
    for (first, _), x in zip(blocks, held):
        outs = finish(first, width, x, swaps.swap_cores(x), total, outs)
    return tuple(outs)


def solution(mesh):
    sizes = dict(mesh.shape)
    split = P(AXES)
    placed = (split, split, split, P(), P(), P(), P(), split)

    def step(*args):
        return body(sizes, *args)

    return jax.shard_map(step, mesh=mesh, in_specs=placed, out_specs=(P(),) * 4, check_vma=False)
```
